512 devices in a mesh: section: 8 (over z_lo), dp: 32 (over x, y, core), tensor: 2 (over z_hi).
Axes of the slice: x: 4, y: 4, z: 16 (z_hi: 2, z_lo: 8; z = z_hi * 8 + z_lo), core: 2. Of those that a mesh axis runs over, the one named last changes fastest.
Arguments:
- hidden_in: bfloat16 [8, 4096, 8192], P('section', ('dp', 'tensor')), may hold values from -600 to 600
- norm_gain: bfloat16 [8, 8192], P('section'), may hold values from 0.5 to 1.5
- value_weight: bfloat16 [8, 8192, 512], P('section', 'dp', 'tensor'), may hold values from -0.0625 to 0.0625
- query_vectors: bfloat16 [8, 4096, 4096], P('section', 'dp', 'tensor'), may hold values from -9 to 9
- key_vectors: bfloat16 [8, 4096, 512], P('section', 'dp', 'tensor'), may hold values from -9 to 9
- grad_attn: bfloat16 [8, 4096, 4096], P('section', 'dp', 'tensor'), may hold values from -250 to 250
- positions: int32 [8, 4096], P('section', 'dp'), may hold values from 0 to 65535, as said below
Outputs:
- value_weight_grad: float32 [8, 8192, 512], P('section', 'dp', 'tensor')
- norm_gain_grad: float32 [8, 8192], P('section')
- to_previous: bfloat16 [8, 4096, 8192], P('section', ('dp', 'tensor'))
The draws below stay inside these ranges and needn't reach their ends.
Inputs may be any that keep to these rules, and one draw needn't show every extreme that they name: Within each micro-batch of 128 rows, positions rise by one from row to row except at one row between row 32 and row 95, where a new document starts at position 0.
All inputs are finite; a program needn't handle non-finite values.
Results may differ from the reference program's by a relative error of at most 0.014.
Values may be sent and summed in bfloat16 or wider, within the bound.
No kernel may reach another device: no remote copies, remote signals or barrier semaphores. Data moves between devices by JAX's collectives and lax.ppermute only.
A program may use at most 64 MiB of HBM per device.

```python
import math
import jax
import jax.numpy as jnp
from jax import lax

D = 8192
HD = 128
KVH = 4
QPK = 8
QH = 32
KV = 512
TOK = 128
DOC = 65536
N_SECTION = 8
N_DP = 32
N_TENSOR = 2


def boundaries(key):
    return jax.random.randint(jax.random.fold_in(key, 101), (N_SECTION, N_DP), TOK // 4, 3 * TOK // 4).astype(jnp.int32)


def draw_positions(key, part):
    starts = boundaries(key)
    offsets = jax.random.randint(jax.random.fold_in(key, 102), (N_SECTION, N_DP), 0, DOC - TOK + 1).astype(jnp.int32)
    offsets = offsets.at[0, 0].set(DOC - starts[0, 0])
    places = jnp.arange(TOK, dtype=jnp.int32)
    first_piece = offsets[:, :, None] + places
    second_piece = places - starts[:, :, None]
    merged = jnp.where(places < starts[:, :, None], first_piece, second_piece)
    return merged.reshape(N_SECTION, N_DP * TOK).astype(jnp.int32)


def draw_query_vectors(key, part):
    shape_full = (N_SECTION, N_DP, TOK, KVH, QPK, HD)
    values = jnp.clip(jax.random.normal(jax.random.fold_in(key, 212), shape_full), -6.0, 6.0)
    return values.reshape(N_SECTION, N_DP * TOK, KVH * QPK * HD).astype(jnp.bfloat16)


def draw_key_vectors(key, part):
    shape_full = (N_SECTION, N_DP, TOK, KVH, HD)
    values = jnp.clip(jax.random.normal(jax.random.fold_in(key, 222), shape_full), -6.0, 6.0)
    return values.reshape(N_SECTION, N_DP * TOK, KVH * HD).astype(jnp.bfloat16)


def draw_grad_attn(key, part):
    shape_full = (N_SECTION, N_DP * TOK, QH * HD)
    rising = 3.0 ** (jnp.arange(N_DP * TOK, dtype=jnp.float32) / (N_DP * TOK))
    values = jnp.clip(jax.random.normal(jax.random.fold_in(key, 303), shape_full), -6.0, 6.0)
    values = values * rising[:, None] * 4.0
    return values.astype(jnp.bfloat16)


def draw_hidden_in(key, part):
    shape_full = (N_SECTION, N_DP * TOK, D)
    values = jnp.clip(jax.random.normal(jax.random.fold_in(key, 404), shape_full), -6.0, 6.0)
    return values.astype(jnp.bfloat16)


def block_scale(rng, extent, shards, least, high):
    def one(axis_at, parts):
        draws = jax.random.uniform(jax.random.fold_in(jax.random.fold_in(rng, 6), axis_at), (parts,), jnp.float32, least / len(shards), high / len(shards))
        return jnp.repeat(jnp.exp(draws), extent[axis_at] // parts).reshape((-1,) + (1,) * (len(extent) - axis_at - 1))

    factor_of = one(*shards[0])
    for cut in shards[1:]:
        factor_of = factor_of * one(*cut)
    return factor_of


def scatter_about(key, dims, deviation, reach, shards=(), kind=jnp.bfloat16):
    array = deviation * jax.random.normal(key, dims, jnp.float32)
    if shards:
        array = array * block_scale(key, dims, shards, -0.22, 0.18)
    return jnp.clip(array, -reach, reach).astype(kind)


def setup_inputs(seed: int = 0) -> dict:
    streams_of = jax.random.split(jax.random.key(seed), 8)
    hidden_in = draw_hidden_in(jax.random.fold_in(streams_of[7], 71), 0)
    norm_gain = jnp.clip(1.0 + 0.1 * jax.random.normal(streams_of[1], (N_SECTION, D), jnp.float32), 0.5, 1.5).astype(jnp.bfloat16)
    value_weight = scatter_about(streams_of[2], (N_SECTION, D, KV), D ** -0.5, 0.0625, ((0, 8), (1, 32), (2, 2)))
    query_vectors = draw_query_vectors(jax.random.fold_in(streams_of[7], 71), 0)
    key_vectors = draw_key_vectors(jax.random.fold_in(streams_of[7], 71), 0)
    grad_attn = draw_grad_attn(jax.random.fold_in(streams_of[7], 71), 0)
    positions = draw_positions(jax.random.fold_in(streams_of[7], 71), 0)
    return dict(hidden_in=hidden_in, norm_gain=norm_gain, value_weight=value_weight, query_vectors=query_vectors, key_vectors=key_vectors, grad_attn=grad_attn, positions=positions)


def attend(operands):
    query_rows, key_rows, grad_rows, position_rows = operands
    length = query_rows.shape[0]
    groups = key_rows.shape[1] // HD
    query_heads = query_rows.astype(jnp.float32).reshape(length, groups, QPK, HD)
    key_heads = key_rows.astype(jnp.float32).reshape(length, groups, HD)
    grad_heads = grad_rows.astype(jnp.float32).reshape(length, groups, QPK, HD)
    scores = jnp.einsum('igpd,jgd->gpij', query_heads, key_heads) / math.sqrt(HD)
    places = jnp.arange(length, dtype=jnp.int32)
    visible = (places[:, None] >= places[None, :]) & (position_rows[:, None] - position_rows[None, :] == places[:, None] - places[None, :])
    masked = jnp.where(visible, scores, jnp.float32(-1e+30))
    largest = lax.optimization_barrier(jnp.max(masked, axis=-1, keepdims=True))
    powers = jnp.where(visible, jnp.exp(masked - largest), jnp.float32(0.0))
    probabilities = powers / lax.optimization_barrier(jnp.sum(powers, axis=-1, keepdims=True))
    weights = lax.optimization_barrier(probabilities.astype(jnp.bfloat16)).astype(jnp.float32)
    value_grad = jnp.einsum('gpij,igpd->jgd', weights, grad_heads)
    return value_grad.reshape(length, groups * HD).astype(jnp.bfloat16)

def one_section(operands):
    hidden_in, norm_gain, value_weight, query_vectors, key_vectors, grad_attn, positions = operands
    rows_float = hidden_in.astype(jnp.float32)
    root_mean = jnp.sqrt(lax.optimization_barrier(jnp.mean(rows_float * rows_float, axis=1, keepdims=True)) + 1e-05)
    normed = rows_float / root_mean
    gain_float = norm_gain.astype(jnp.float32)
    layer_input = (normed * gain_float).astype(jnp.bfloat16)

    def batched(stacked):
        return stacked.reshape((N_DP, TOK) + stacked.shape[1:])
    value_grad = lax.map(attend, (batched(query_vectors), batched(key_vectors), batched(grad_attn), batched(positions)))

    def add_term(running, pieces):
        inputs, gradients = pieces
        partial_term = jnp.dot(inputs.T, gradients, preferred_element_type=jnp.float32).astype(jnp.bfloat16)
        return (running + lax.optimization_barrier(partial_term).astype(jnp.float32), None)
    weight_grad, _ = lax.scan(add_term, jnp.zeros((D, KV), jnp.float32), (batched(layer_input), value_grad))
    value_flat = value_grad.reshape(N_DP * TOK, KV)
    group_width = KV // N_TENSOR
    grad_input = jnp.zeros((N_DP * TOK, D), jnp.float32)
    for column_group in range(N_TENSOR):
        first_column = column_group * group_width
        partial_term = jnp.dot(value_flat[:, first_column:first_column + group_width], value_weight[:, first_column:first_column + group_width].T, preferred_element_type=jnp.float32).astype(jnp.bfloat16)
        grad_input = grad_input + lax.optimization_barrier(partial_term).astype(jnp.float32)
    gain_grad = lax.optimization_barrier(jnp.sum(grad_input * normed, axis=0))
    grad_normed = grad_input * gain_float
    inner_mean = lax.optimization_barrier(jnp.mean(grad_normed * normed, axis=1, keepdims=True))
    grad_hidden = ((grad_normed - normed * inner_mean) / root_mean).astype(jnp.bfloat16)
    return (weight_grad, gain_grad, grad_hidden)

def reference(hidden_in, norm_gain, value_weight, query_vectors, key_vectors, grad_attn, positions):
    weight_grad, gain_grad, grad_hidden = lax.map(one_section, (hidden_in, norm_gain, value_weight, query_vectors, key_vectors, grad_attn, positions))
    to_previous = jnp.concatenate([grad_hidden[1:], jnp.zeros_like(grad_hidden[:1])], axis=0)
    return (weight_grad, gain_grad, to_previous)
```

```python
import math

import jax
import jax.numpy as jnp
from jax import lax
from jax.sharding import PartitionSpec as P


HD = 128
QPK = 8


def shifted(value, axis, steps):
    count = lax.axis_size(axis)
    first, last = (max(0, -steps), min(count, count - steps))
    return lax.ppermute(value, axis, [(source, source + steps) for source in range(first, last)])


def swapped(value):
    return lax.ppermute(value, "tensor", [(0, 1), (1, 0)])


def exchanged(value, split, joined):
    return lax.all_to_all(value, "dp", split, joined)


def gathered(value):
    count = lax.axis_size("dp")
    copies = jnp.broadcast_to(value[None], (count,) + value.shape)
    return exchanged(copies, 0, 0)


def attend(query_rows, key_rows, grad_rows, position_rows):
    length = query_rows.shape[0]
    groups = key_rows.shape[1] // HD
    query_heads = query_rows.reshape(length, groups, QPK, HD)
    key_heads = key_rows.reshape(length, groups, HD)
    grad_heads = grad_rows.reshape(length, groups, QPK, HD)
    scores = jnp.einsum(
        "igpd,jgd->gpij", query_heads, key_heads, preferred_element_type=jnp.float32
    ) / math.sqrt(HD)
    places = jnp.arange(length, dtype=jnp.int32)
    visible = (places[:, None] >= places[None, :]) & (
        position_rows[:, None] - position_rows[None, :] == places[:, None] - places[None, :]
    )
    masked = jnp.where(visible, scores, jnp.float32(-1e30))
    largest = jnp.max(masked, axis=-1, keepdims=True)
    powers = jnp.where(visible, jnp.exp(masked - largest), jnp.float32(0.0))
    probabilities = powers / jnp.sum(powers, axis=-1, keepdims=True)
    weights = probabilities.astype(jnp.bfloat16)
    value_grad = jnp.einsum(
        "gpij,igpd->jgd", weights, grad_heads, preferred_element_type=jnp.float32
    )
    return value_grad.reshape(length, groups * HD).astype(jnp.bfloat16)


def layer(hidden_in, norm_gain, value_weight, query_vectors, key_vectors, grad_attn, positions):
    n_dp = lax.axis_size("dp")
    here = lax.axis_index("dp")
    half = lax.axis_index("tensor")
    own_rows, width = hidden_in.shape[1:]
    chunk = width // n_dp
    local_weight = value_weight[0]
    own_columns = local_weight.shape[1]
    other_weight = swapped(local_weight)
    rows_float = hidden_in[0].astype(jnp.float32)
    root_mean = jnp.sqrt(jnp.mean(rows_float * rows_float, axis=1, keepdims=True) + 1e-05)
    normed = rows_float / root_mean
    normed_columns = exchanged(
        normed.astype(jnp.bfloat16).reshape(own_rows, n_dp, chunk), 1, 0
    ).reshape(n_dp * own_rows, chunk)
    value_grad = attend(query_vectors[0], key_vectors[0], grad_attn[0], positions[0])
    kept = lax.dynamic_slice_in_dim(value_grad, half * own_rows, own_rows, 0)
    given = lax.dynamic_slice_in_dim(value_grad, (1 - half) * own_rows, own_rows, 0)
    own_value = jnp.concatenate([kept, swapped(given)], axis=1)
    plane_value = gathered(own_value).reshape(n_dp * own_rows, 2 * own_columns)
    full_weight = jnp.concatenate([local_weight, other_weight], axis=1)
    grad_columns = jnp.einsum(
        "tk,ck->tc", plane_value, full_weight, preferred_element_type=jnp.float32
    ).astype(jnp.bfloat16)
    own_grad = (
        exchanged(grad_columns.reshape(n_dp, own_rows, chunk), 0, 1)
        .reshape(own_rows, width)
        .astype(jnp.float32)
    )
    normed_term = jnp.einsum(
        "tc,tk->ck", normed_columns, plane_value, preferred_element_type=jnp.float32
    )
    gain_float = norm_gain[0].astype(jnp.float32)
    own_gain = lax.dynamic_slice_in_dim(gain_float, here * chunk, chunk, 0)
    term = normed_term * own_gain[:, None]
    weight_grad = term[:, :own_columns] + swapped(
        term[:, own_columns:].astype(jnp.bfloat16)
    ).astype(jnp.float32)
    gain_term = jnp.sum(normed_term * full_weight.astype(jnp.float32), axis=1)
    gain_grad = gathered(gain_term + swapped(gain_term)).reshape(width)
    grad_normed = own_grad * gain_float
    inner_mean = jnp.mean(grad_normed * normed, axis=1, keepdims=True)
    grad_hidden = ((grad_normed - normed * inner_mean) / root_mean).astype(jnp.bfloat16)
    to_previous = shifted(grad_hidden, "section", -1)
    return (weight_grad[None], gain_grad[None], to_previous[None])


def solution(mesh):
    placed = (
        P("section", ("dp", "tensor"), None),
        P("section", None),
        P("section", "dp", "tensor"),
        P("section", "dp", "tensor"),
        P("section", "dp", "tensor"),
        P("section", "dp", "tensor"),
        P("section", "dp"),
    )
    return jax.shard_map(
        layer,
        mesh=mesh,
        in_specs=placed,
        out_specs=(
            P("section", "dp", "tensor"),
            P("section", None),
            P("section", ("dp", "tensor"), None),
        ),
        check_vma=False,
    )
```

```python
import math

import jax
import jax.numpy as jnp
from jax import lax
from jax.sharding import PartitionSpec as P


HD = 128
QPK = 8


def shifted(value, axis, steps):
    count = lax.axis_size(axis)
    first, last = (max(0, -steps), min(count, count - steps))
    return lax.ppermute(value, axis, [(source, source + steps) for source in range(first, last)])


def swapped(value):
    return lax.ppermute(value, "tensor", [(0, 1), (1, 0)])


def same_core():
    count = lax.axis_size("dp")
    return [list(range(core, count, 2)) for core in range(2)]


def exchanged(value, split, joined):
    return lax.all_to_all(value, "dp", split, joined, axis_index_groups=same_core())


def gathered(value):
    count = lax.axis_size("dp") // 2
    copies = jnp.broadcast_to(value[None], (count,) + value.shape)
    return exchanged(copies, 0, 0)


def other_core(value):
    count = lax.axis_size("dp")
    return lax.ppermute(value, "dp", [(source, source ^ 1) for source in range(count)])


def by_core(core, own, other):
    first = jnp.where(core == 0, own, other)
    second = jnp.where(core == 0, other, own)
    return jnp.concatenate([first, second], axis=0)


def attend(query_rows, key_rows, grad_rows, position_rows):
    length = query_rows.shape[0]
    groups = key_rows.shape[1] // HD
    query_heads = query_rows.reshape(length, groups, QPK, HD)
    key_heads = key_rows.reshape(length, groups, HD)
    grad_heads = grad_rows.reshape(length, groups, QPK, HD)
    scores = jnp.einsum(
        "igpd,jgd->gpij", query_heads, key_heads, preferred_element_type=jnp.float32
    ) / math.sqrt(HD)
    places = jnp.arange(length, dtype=jnp.int32)
    visible = (places[:, None] >= places[None, :]) & (
        position_rows[:, None] - position_rows[None, :] == places[:, None] - places[None, :]
    )
    masked = jnp.where(visible, scores, jnp.float32(-1e30))
    largest = jnp.max(masked, axis=-1, keepdims=True)
    powers = jnp.where(visible, jnp.exp(masked - largest), jnp.float32(0.0))
    probabilities = powers / jnp.sum(powers, axis=-1, keepdims=True)
    weights = probabilities.astype(jnp.bfloat16)
    value_grad = jnp.einsum(
        "gpij,igpd->jgd", weights, grad_heads, preferred_element_type=jnp.float32
    )
    return value_grad.reshape(length, groups * HD).astype(jnp.bfloat16)


def layer(hidden_in, norm_gain, value_weight, query_vectors, key_vectors, grad_attn, positions):
    n_dp = lax.axis_size("dp")
    n_chip = n_dp // 2
    here = lax.axis_index("dp")
    core = here % 2
    half = lax.axis_index("tensor")
    own_rows, width = hidden_in.shape[1:]
    chunk = width // n_dp
    local_weight = value_weight[0]
    own_columns = local_weight.shape[1]
    rows_float = hidden_in[0].astype(jnp.float32)
    root_mean = jnp.sqrt(jnp.mean(rows_float * rows_float, axis=1, keepdims=True) + 1e-05)
    normed = rows_float / root_mean
    normed_columns = exchanged(
        normed.astype(jnp.bfloat16).reshape(own_rows, n_chip, 2 * chunk), 1, 0
    ).reshape(n_chip * own_rows, 2 * chunk)
    value_grad = attend(query_vectors[0], key_vectors[0], grad_attn[0], positions[0])
    kept = lax.dynamic_slice_in_dim(value_grad, half * own_rows, own_rows, 0)
    given = lax.dynamic_slice_in_dim(value_grad, (1 - half) * own_rows, own_rows, 0)
    own_value = jnp.concatenate([kept, swapped(given)], axis=1)
    device_weight = jnp.concatenate([local_weight, swapped(local_weight)], axis=1)
    full_weight = by_core(core, device_weight, other_core(device_weight))
    group_value = gathered(own_value).reshape(n_chip * own_rows, 2 * own_columns)
    grad_columns = jnp.einsum(
        "tk,ck->tc", group_value, full_weight, preferred_element_type=jnp.float32
    ).astype(jnp.bfloat16)
    own_grad = (
        exchanged(grad_columns.reshape(n_chip, own_rows, 2 * chunk), 0, 1)
        .reshape(own_rows, width)
        .astype(jnp.float32)
    )
    group_term = jnp.einsum(
        "tc,tk->ck", normed_columns, group_value, preferred_element_type=jnp.float32
    )
    kept_term = lax.dynamic_slice_in_dim(group_term, core * chunk, chunk, 0)
    given_term = lax.dynamic_slice_in_dim(group_term, (1 - core) * chunk, chunk, 0)
    plane_term = kept_term + other_core(given_term.astype(jnp.bfloat16)).astype(jnp.float32)
    gain_term = jnp.sum(plane_term * device_weight.astype(jnp.float32), axis=1)
    gain_high = lax.reduce_precision(gain_term, 8, 7)
    gain_low = gain_term - gain_high
    sent_term = jnp.concatenate(
        [
            plane_term[:, own_columns:].astype(jnp.bfloat16),
            jnp.pad(
                jnp.stack([gain_high, gain_low]).astype(jnp.bfloat16), ((0, 14), (0, 0))
            ),
        ],
        axis=0,
    )
    given_back = swapped(sent_term).astype(jnp.float32)
    gain_float = norm_gain[0].astype(jnp.float32)
    own_gain = lax.dynamic_slice_in_dim(gain_float, here * chunk, chunk, 0)
    weight_grad = (plane_term[:, :own_columns] + given_back[:chunk]) * own_gain[:, None]
    gain_chunk = gain_high + gain_low + given_back[chunk] + given_back[chunk + 1]
    gain_grad = lax.all_to_all(
        jnp.broadcast_to(gain_chunk[None], (n_dp, chunk)), "dp", 0, 0
    ).reshape(width)
    grad_normed = own_grad * gain_float
    inner_mean = jnp.mean(grad_normed * normed, axis=1, keepdims=True)
    grad_hidden = ((grad_normed - normed * inner_mean) / root_mean).astype(jnp.bfloat16)
    to_previous = shifted(grad_hidden, "section", -1)
    return (weight_grad[None], gain_grad[None], to_previous[None])


def solution(mesh):
    placed = (
        P("section", ("dp", "tensor"), None),
        P("section", None),
        P("section", "dp", "tensor"),
        P("section", "dp", "tensor"),
        P("section", "dp", "tensor"),
        P("section", "dp", "tensor"),
        P("section", "dp"),
    )
    return jax.shard_map(
        layer,
        mesh=mesh,
        in_specs=placed,
        out_specs=(
            P("section", "dp", "tensor"),
            P("section", None),
            P("section", ("dp", "tensor"), None),
        ),
        check_vma=False,
    )
```

```python
import math

import jax
import jax.numpy as jnp
from jax import lax
from jax.sharding import PartitionSpec as P


HD = 128
QPK = 8


def along(value, steps):
    half = lax.axis_size("section")
    count = 2 * half
    place = [(plane % half) * 2 + plane // half for plane in range(count)]
    pairs = [(place[plane], place[(plane + steps) % count]) for plane in range(count)]
    return lax.ppermute(value, ("section", "tensor"), pairs)


def same_core():
    count = lax.axis_size("dp")
    return [list(range(core, count, 2)) for core in range(2)]


def exchanged(value, split, joined):
    return lax.all_to_all(value, "dp", split, joined, axis_index_groups=same_core())


def gathered(value):
    count = lax.axis_size("dp") // 2
    copies = jnp.broadcast_to(value[None], (count,) + value.shape)
    return exchanged(copies, 0, 0)


def other_core(value):
    count = lax.axis_size("dp")
    return lax.ppermute(value, "dp", [(source, source ^ 1) for source in range(count)])


def by_core(core, own, other):
    first = jnp.where(core == 0, own, other)
    second = jnp.where(core == 0, other, own)
    return jnp.concatenate([first, second], axis=0)


def attend(query_rows, key_rows, grad_rows, position_rows):
    length = query_rows.shape[0]
    groups = key_rows.shape[1] // HD
    query_heads = query_rows.reshape(length, groups, QPK, HD)
    key_heads = key_rows.reshape(length, groups, HD)
    grad_heads = grad_rows.reshape(length, groups, QPK, HD)
    scores = jnp.einsum(
        "igpd,jgd->gpij", query_heads, key_heads, preferred_element_type=jnp.float32
    ) / math.sqrt(HD)
    places = jnp.arange(length, dtype=jnp.int32)
    visible = (places[:, None] >= places[None, :]) & (
        position_rows[:, None] - position_rows[None, :] == places[:, None] - places[None, :]
    )
    masked = jnp.where(visible, scores, jnp.float32(-1e30))
    largest = jnp.max(masked, axis=-1, keepdims=True)
    powers = jnp.where(visible, jnp.exp(masked - largest), jnp.float32(0.0))
    probabilities = powers / jnp.sum(powers, axis=-1, keepdims=True)
    weights = probabilities.astype(jnp.bfloat16)
    value_grad = jnp.einsum(
        "gpij,igpd->jgd", weights, grad_heads, preferred_element_type=jnp.float32
    )
    return value_grad.reshape(length, groups * HD).astype(jnp.bfloat16)


def statistics(rows):
    rows_float = rows.astype(jnp.float32)
    root_mean = jnp.sqrt(jnp.mean(rows_float * rows_float, axis=1, keepdims=True) + 1e-05)
    return rows_float / root_mean, root_mean


def layer(hidden_in, norm_gain, value_weight, query_vectors, key_vectors, grad_attn, positions):
    n_dp = lax.axis_size("dp")
    n_chip = n_dp // 2
    n_section = lax.axis_size("section")
    here = lax.axis_index("dp")
    core = here % 2
    half = lax.axis_index("tensor")
    own_rows, width = hidden_in.shape[1:]
    chunk = width // n_dp
    local_weight = value_weight[0]
    own_columns = local_weight.shape[1]
    across = n_section - 1
    work_hidden = along(hidden_in[0], -1)
    normed, _ = statistics(hidden_in[0])
    home_columns = exchanged(
        normed.astype(jnp.bfloat16).reshape(own_rows, n_chip, 2 * chunk), 1, 0
    ).reshape(n_chip * own_rows, 2 * chunk)
    normed_columns = along(home_columns, -1)
    value_grad = attend(query_vectors[0], key_vectors[0], grad_attn[0], positions[0])
    kept = lax.dynamic_slice_in_dim(value_grad, half * own_rows, own_rows, 0)
    given = lax.dynamic_slice_in_dim(value_grad, (1 - half) * own_rows, own_rows, 0)
    work_value = jnp.concatenate([along(kept, -1), along(given, across)], axis=1)
    device_weight = jnp.concatenate(
        [along(local_weight, -1), along(local_weight, across)],
        axis=1,
    )
    full_weight = by_core(core, device_weight, other_core(device_weight))
    group_value = gathered(work_value).reshape(n_chip * own_rows, 2 * own_columns)
    grad_columns = jnp.einsum(
        "tk,ck->tc", group_value, full_weight, preferred_element_type=jnp.float32
    ).astype(jnp.bfloat16)
    own_grad = (
        exchanged(grad_columns.reshape(n_chip, own_rows, 2 * chunk), 0, 1)
        .reshape(own_rows, width)
        .astype(jnp.float32)
    )
    group_term = jnp.einsum(
        "tc,tk->ck", normed_columns, group_value, preferred_element_type=jnp.float32
    )
    group_sum = jnp.sum(group_term * full_weight.astype(jnp.float32), axis=1)
    home_sum = along(group_sum, 1) + along(group_sum, -across)
    all_sums = lax.all_to_all(
        jnp.broadcast_to(home_sum[None], (n_dp, 2 * chunk)), "dp", 0, 0
    )
    gain_grad = jnp.sum(all_sums.reshape(n_chip, 2, 2 * chunk), axis=1).reshape(width)
    kept_term = lax.dynamic_slice_in_dim(group_term, core * chunk, chunk, 0)
    given_term = lax.dynamic_slice_in_dim(group_term, (1 - core) * chunk, chunk, 0)
    plane_term = kept_term + other_core(given_term.astype(jnp.bfloat16)).astype(jnp.float32)
    sent_term = plane_term.astype(jnp.bfloat16)
    home_term = along(sent_term[:, :own_columns], 1).astype(jnp.float32) + along(
        sent_term[:, own_columns:], -across
    ).astype(jnp.float32)
    own_gain = lax.dynamic_slice_in_dim(norm_gain[0], here * chunk, chunk, 0)
    weight_grad = home_term * own_gain.astype(jnp.float32)[:, None]
    work_gain = along(norm_gain[0], -1).astype(jnp.float32)
    work_normed, root_mean = statistics(work_hidden)
    last = lax.axis_index("section") == n_section - 1
    grad_normed = own_grad * work_gain
    inner_mean = jnp.mean(grad_normed * work_normed, axis=1, keepdims=True)
    grad_hidden = (grad_normed - work_normed * inner_mean) / root_mean
    to_previous = jnp.where(last, jnp.float32(0.0), grad_hidden).astype(jnp.bfloat16)
    return (weight_grad[None], gain_grad[None], to_previous[None])


def solution(mesh):
    placed = (
        P("section", ("dp", "tensor"), None),
        P("section", None),
        P("section", "dp", "tensor"),
        P("section", "dp", "tensor"),
        P("section", "dp", "tensor"),
        P("section", "dp", "tensor"),
        P("section", "dp"),
    )
    return jax.shard_map(
        layer,
        mesh=mesh,
        in_specs=placed,
        out_specs=(
            P("section", "dp", "tensor"),
            P("section", None),
            P("section", ("dp", "tensor"), None),
        ),
        check_vma=False,
    )
```

```python
import math

import jax
import jax.numpy as jnp
from jax import lax
from jax.experimental import pallas as pl
from jax.experimental.pallas import tpu as pltpu
from jax.sharding import PartitionSpec as P


HD = 128
QPK = 8


def along(value, steps):
    half = lax.axis_size("section")
    count = 2 * half
    place = [(plane % half) * 2 + plane // half for plane in range(count)]
    pairs = [(place[plane], place[(plane + steps) % count]) for plane in range(count)]
    return lax.ppermute(value, ("section", "tensor"), pairs)


def same_core():
    count = lax.axis_size("dp")
    return [list(range(core, count, 2)) for core in range(2)]


def exchanged(value, split, joined):
    return lax.all_to_all(value, "dp", split, joined, axis_index_groups=same_core())


def gathered(value):
    count = lax.axis_size("dp") // 2
    copies = jnp.broadcast_to(value[None], (count,) + value.shape)
    return exchanged(copies, 0, 0)


def other_core(value):
    count = lax.axis_size("dp")
    return lax.ppermute(value, "dp", [(source, source ^ 1) for source in range(count)])


def by_core(core, own, other):
    first = jnp.where(core == 0, own, other)
    second = jnp.where(core == 0, other, own)
    return jnp.concatenate([first, second], axis=0)


def whole(memory=pltpu.VMEM):
    return pl.BlockSpec(memory_space=memory)


def norm_kernel(hidden_ref, normed_ref):
    rows = hidden_ref[...].astype(jnp.float32)
    root_mean = jnp.sqrt(jnp.mean(rows * rows, axis=1, keepdims=True) + 1e-05)
    normed = (rows / root_mean).astype(jnp.bfloat16)
    count, _, columns = normed_ref.shape
    for place in range(count):
        normed_ref[place] = normed[:, place * columns : (place + 1) * columns]


def normed_blocks(rows, count):
    length, width = rows.shape
    return pl.pallas_call(
        norm_kernel,
        out_shape=jax.ShapeDtypeStruct((count, length, width // count), jnp.bfloat16),
        in_specs=[whole()],
        out_specs=whole(),
    )(rows)


def attend_kernel(half_ref, query_ref, key_ref, grad_ref, position_ref, kept_ref, given_ref, scratch_ref):
    length = query_ref.shape[0]
    groups = key_ref.shape[1] // HD
    seen_row = lax.broadcasted_iota(jnp.int32, (length, length), 0)
    query_row = lax.broadcasted_iota(jnp.int32, (length, length), 1)
    query_start = jnp.broadcast_to(position_ref[...], (length, length)) - query_row
    seen_start = query_start.T
    visible = (seen_row <= query_row) & (query_start == seen_start)
    for group in range(groups):
        keys = key_ref[:, group * HD : (group + 1) * HD]
        total = jnp.zeros((length, HD), jnp.float32)
        for head in range(group * QPK, (group + 1) * QPK):
            queries = query_ref[:, head * HD : (head + 1) * HD]
            scores = lax.dot_general(
                keys, queries, (((1,), (1,)), ((), ())), preferred_element_type=jnp.float32
            ) * (1.0 / math.sqrt(HD))
            masked = jnp.where(visible, scores, jnp.float32(-1e30))
            largest = jnp.max(masked, axis=0, keepdims=True)
            powers = jnp.where(visible, jnp.exp(masked - largest), jnp.float32(0.0))
            weights = powers / jnp.sum(powers, axis=0, keepdims=True)
            total += lax.dot_general(
                weights.astype(jnp.bfloat16),
                grad_ref[:, head * HD : (head + 1) * HD],
                (((1,), (0,)), ((), ())),
                preferred_element_type=jnp.float32,
            )
        scratch_ref[:, group * HD : (group + 1) * HD] = total
    rows = kept_ref.shape[0]
    half = half_ref[0]
    kept_ref[...] = scratch_ref[pl.ds(half * rows, rows), :].astype(jnp.bfloat16)
    given_ref[...] = scratch_ref[pl.ds((1 - half) * rows, rows), :].astype(jnp.bfloat16)


def attend(half, query_rows, key_rows, grad_rows, position_rows):
    length, columns = key_rows.shape
    part = jax.ShapeDtypeStruct((length // 2, columns), jnp.bfloat16)
    return pl.pallas_call(
        attend_kernel,
        out_shape=(part, part),
        in_specs=[whole(pltpu.SMEM)] + [whole()] * 4,
        out_specs=(whole(), whole()),
        scratch_shapes=[pltpu.VMEM((length, columns), jnp.float32)],
    )(half[None], query_rows, key_rows, grad_rows, position_rows)


def finish_kernel(last_ref, grad_ref, hidden_ref, result_ref):
    rows = hidden_ref[...].astype(jnp.float32)
    root_mean = jnp.sqrt(jnp.mean(rows * rows, axis=1, keepdims=True) + 1e-05)
    count, _, columns = grad_ref.shape
    total = jnp.zeros_like(root_mean)
    for place in range(count):
        block = rows[:, place * columns : (place + 1) * columns] / root_mean
        total += jnp.sum(grad_ref[place].astype(jnp.float32) * block, axis=1, keepdims=True)
    inner_mean = total / rows.shape[1]
    for place in range(count):
        part = pl.ds(place * columns, columns)
        normed = rows[:, place * columns : (place + 1) * columns] / root_mean
        grad_hidden = (grad_ref[place].astype(jnp.float32) - normed * inner_mean) / root_mean
        result_ref[:, part] = jnp.where(last_ref[0] != 0, jnp.float32(0.0), grad_hidden).astype(
            jnp.bfloat16
        )


def finished(last, grad_blocks, rows):
    return pl.pallas_call(
        finish_kernel,
        out_shape=jax.ShapeDtypeStruct(rows.shape, jnp.bfloat16),
        in_specs=[whole(pltpu.SMEM), whole(), whole()],
        out_specs=whole(),
    )(last.astype(jnp.int32)[None], grad_blocks, rows)


def layer(hidden_in, norm_gain, value_weight, query_vectors, key_vectors, grad_attn, positions):
    n_dp = lax.axis_size("dp")
    n_chip = n_dp // 2
    n_section = lax.axis_size("section")
    here = lax.axis_index("dp")
    core = here % 2
    half = lax.axis_index("tensor")
    own_rows, width = hidden_in.shape[1:]
    chunk = width // n_dp
    local_weight = value_weight[0]
    own_columns = local_weight.shape[1]
    across = n_section - 1
    own_gain = lax.dynamic_slice_in_dim(norm_gain[0], here * chunk, chunk, 0)
    gained_weight = jnp.concatenate(
        [local_weight, jnp.broadcast_to(own_gain.reshape(1, -1), (16, own_columns))], axis=0
    )
    work_weight = along(gained_weight, -1)
    other_weight = along(local_weight, across)
    normed = normed_blocks(hidden_in[0], n_chip)
    home_columns = exchanged(normed, 0, 0).reshape(n_chip * own_rows, 2 * chunk)
    work_hidden = along(hidden_in[0], -1)
    kept, given = attend(half, query_vectors[0], key_vectors[0], grad_attn[0], positions)
    work_value = jnp.concatenate([along(kept, -1), along(given, across)], axis=1)
    normed_columns = along(home_columns, -1)
    device_weight = jnp.concatenate(
        [
            jnp.concatenate([work_weight[:chunk], other_weight], axis=1),
            jnp.concatenate([work_weight[chunk:], work_weight[chunk:]], axis=1),
        ],
        axis=0,
    )
    swapped_weight = other_core(device_weight)
    full_weight = by_core(core, device_weight[:chunk], swapped_weight[:chunk])
    work_gain = by_core(
        core, device_weight[chunk, :own_columns], swapped_weight[chunk, :own_columns]
    ).astype(jnp.float32)
    group_value = gathered(work_value).reshape(n_chip * own_rows, 2 * own_columns)
    group_term = jnp.einsum(
        "tc,tk->ck", normed_columns, group_value, preferred_element_type=jnp.float32
    )
    group_sum = jnp.sum(group_term * full_weight.astype(jnp.float32), axis=1)
    kept_term = lax.dynamic_slice_in_dim(group_term, core * chunk, chunk, 0)
    given_term = lax.dynamic_slice_in_dim(group_term, (1 - core) * chunk, chunk, 0)
    plane_term = kept_term + other_core(given_term.astype(jnp.bfloat16)).astype(jnp.float32)
    grad_columns = (
        jnp.einsum("tk,ck->tc", group_value, full_weight, preferred_element_type=jnp.float32)
        * work_gain
    ).astype(jnp.bfloat16)
    grad_blocks = exchanged(grad_columns.reshape(n_chip, own_rows, 2 * chunk), 0, 0)
    sent_term = plane_term.astype(jnp.bfloat16)
    home_term = along(sent_term[:, :own_columns], 1).astype(jnp.float32) + along(
        sent_term[:, own_columns:], -across
    ).astype(jnp.float32)
    weight_grad = home_term * own_gain.astype(jnp.float32)[:, None]
    home_sum = along(group_sum, 1) + along(group_sum, -across)
    all_sums = lax.all_to_all(
        jnp.broadcast_to(home_sum[None], (n_dp, 2 * chunk)), "dp", 0, 0
    )
    gain_grad = jnp.sum(all_sums.reshape(n_chip, 2, 2 * chunk), axis=1).reshape(width)
    to_previous = finished(
        lax.axis_index("section") == n_section - 1, grad_blocks, work_hidden
    )
    return (weight_grad[None], gain_grad[None], to_previous[None])


def solution(mesh):
    placed = (
        P("section", ("dp", "tensor"), None),
        P("section", None),
        P("section", "dp", "tensor"),
        P("section", "dp", "tensor"),
        P("section", "dp", "tensor"),
        P("section", "dp", "tensor"),
        P("section", "dp"),
    )
    return jax.shard_map(
        layer,
        mesh=mesh,
        in_specs=placed,
        out_specs=(
            P("section", "dp", "tensor"),
            P("section", None),
            P("section", ("dp", "tensor"), None),
        ),
        check_vma=False,
    )
```

```python
import math

import jax
import jax.numpy as jnp
from jax import lax
from jax.experimental import pallas as pl
from jax.experimental.pallas import tpu as pltpu
from jax.sharding import PartitionSpec as P


HD = 128
QPK = 8


def shifted(value, axis, steps):
    count = lax.axis_size(axis)
    first, last = (max(0, -steps), min(count, count - steps))
    return lax.ppermute(value, axis, [(source, source + steps) for source in range(first, last)])


def swapped(value):
    return lax.ppermute(value, "tensor", [(0, 1), (1, 0)])


def same_core():
    count = lax.axis_size("dp")
    return [list(range(core, count, 2)) for core in range(2)]


def exchanged(value, split, joined):
    return lax.all_to_all(value, "dp", split, joined, axis_index_groups=same_core())


def gathered(value):
    count = lax.axis_size("dp") // 2
    copies = jnp.broadcast_to(value[None], (count,) + value.shape)
    return exchanged(copies, 0, 0)


def other_core(value):
    count = lax.axis_size("dp")
    return lax.ppermute(value, "dp", [(source, source ^ 1) for source in range(count)])


def by_core(core, own, other):
    first = jnp.where(core == 0, own, other)
    second = jnp.where(core == 0, other, own)
    return jnp.concatenate([first, second], axis=0)


def whole(memory=pltpu.VMEM):
    return pl.BlockSpec(memory_space=memory)


def norm_kernel(hidden_ref, normed_ref):
    rows = hidden_ref[...].astype(jnp.float32)
    root_mean = jnp.sqrt(jnp.mean(rows * rows, axis=1, keepdims=True) + 1e-05)
    normed = (rows / root_mean).astype(jnp.bfloat16)
    count, _, columns = normed_ref.shape
    for place in range(count):
        normed_ref[place] = normed[:, place * columns : (place + 1) * columns]


def normed_blocks(rows, count):
    length, width = rows.shape
    return pl.pallas_call(
        norm_kernel,
        out_shape=jax.ShapeDtypeStruct((count, length, width // count), jnp.bfloat16),
        in_specs=[whole()],
        out_specs=whole(),
    )(rows)


def attend_kernel(half_ref, query_ref, key_ref, grad_ref, position_ref, kept_ref, given_ref, scratch_ref):
    length = query_ref.shape[0]
    groups = key_ref.shape[1] // HD
    seen_row = lax.broadcasted_iota(jnp.int32, (length, length), 0)
    query_row = lax.broadcasted_iota(jnp.int32, (length, length), 1)
    query_start = jnp.broadcast_to(position_ref[...], (length, length)) - query_row
    seen_start = query_start.T
    visible = (seen_row <= query_row) & (query_start == seen_start)
    for group in range(groups):
        keys = key_ref[:, group * HD : (group + 1) * HD]
        total = jnp.zeros((length, HD), jnp.float32)
        for head in range(group * QPK, (group + 1) * QPK):
            queries = query_ref[:, head * HD : (head + 1) * HD]
            scores = lax.dot_general(
                keys, queries, (((1,), (1,)), ((), ())), preferred_element_type=jnp.float32
            ) * (1.0 / math.sqrt(HD))
            masked = jnp.where(visible, scores, jnp.float32(-1e30))
            largest = jnp.max(masked, axis=0, keepdims=True)
            powers = jnp.where(visible, jnp.exp(masked - largest), jnp.float32(0.0))
            weights = powers / jnp.sum(powers, axis=0, keepdims=True)
            total += lax.dot_general(
                weights.astype(jnp.bfloat16),
                grad_ref[:, head * HD : (head + 1) * HD],
                (((1,), (0,)), ((), ())),
                preferred_element_type=jnp.float32,
            )
        scratch_ref[:, group * HD : (group + 1) * HD] = total
    rows = kept_ref.shape[0]
    half = half_ref[0]
    kept_ref[...] = scratch_ref[pl.ds(half * rows, rows), :].astype(jnp.bfloat16)
    given_ref[...] = scratch_ref[pl.ds((1 - half) * rows, rows), :].astype(jnp.bfloat16)


def attend(half, query_rows, key_rows, grad_rows, position_rows):
    length, columns = key_rows.shape
    part = jax.ShapeDtypeStruct((length // 2, columns), jnp.bfloat16)
    return pl.pallas_call(
        attend_kernel,
        out_shape=(part, part),
        in_specs=[whole(pltpu.SMEM)] + [whole()] * 4,
        out_specs=(whole(), whole()),
        scratch_shapes=[pltpu.VMEM((length, columns), jnp.float32)],
    )(half[None], query_rows, key_rows, grad_rows, position_rows)


def finish_kernel(grad_ref, hidden_ref, result_ref):
    rows = hidden_ref[...].astype(jnp.float32)
    root_mean = jnp.sqrt(jnp.mean(rows * rows, axis=1, keepdims=True) + 1e-05)
    count, _, columns = grad_ref.shape
    total = jnp.zeros_like(root_mean)
    for place in range(count):
        block = rows[:, place * columns : (place + 1) * columns] / root_mean
        total += jnp.sum(grad_ref[place].astype(jnp.float32) * block, axis=1, keepdims=True)
    inner_mean = total / rows.shape[1]
    for place in range(count):
        part = pl.ds(place * columns, columns)
        normed = rows[:, place * columns : (place + 1) * columns] / root_mean
        grad_hidden = (grad_ref[place].astype(jnp.float32) - normed * inner_mean) / root_mean
        result_ref[:, part] = grad_hidden.astype(jnp.bfloat16)


def finished(grad_blocks, rows):
    return pl.pallas_call(
        finish_kernel,
        out_shape=jax.ShapeDtypeStruct(rows.shape, jnp.bfloat16),
        in_specs=[whole(), whole()],
        out_specs=whole(),
    )(grad_blocks, rows)


def layer(hidden_in, norm_gain, value_weight, query_vectors, key_vectors, grad_attn, positions):
    n_dp = lax.axis_size("dp")
    n_chip = n_dp // 2
    here = lax.axis_index("dp")
    chip = here // 2
    core = here % 2
    half = lax.axis_index("tensor")
    own_rows, width = hidden_in.shape[1:]
    chunk = width // n_dp
    local_weight = value_weight[0]
    own_columns = local_weight.shape[1]
    normed = normed_blocks(hidden_in[0], n_chip)
    normed_columns = exchanged(normed, 0, 0).reshape(n_chip * own_rows, 2 * chunk)
    kept, given = attend(half, query_vectors[0], key_vectors[0], grad_attn[0], positions)
    own_value = jnp.concatenate([kept, swapped(given)], axis=1)
    device_weight = jnp.concatenate([local_weight, swapped(local_weight)], axis=1)
    full_weight = by_core(core, device_weight, other_core(device_weight))
    chip_gain = lax.dynamic_slice_in_dim(norm_gain[0], chip * 2 * chunk, 2 * chunk, 0)
    own_gain = lax.dynamic_slice_in_dim(norm_gain[0], here * chunk, chunk, 0)
    group_value = gathered(own_value).reshape(n_chip * own_rows, 2 * own_columns)
    grad_columns = (
        jnp.einsum("tk,ck->tc", group_value, full_weight, preferred_element_type=jnp.float32)
        * chip_gain.astype(jnp.float32)
    ).astype(jnp.bfloat16)
    grad_blocks = exchanged(grad_columns.reshape(n_chip, own_rows, 2 * chunk), 0, 0)
    group_term = jnp.einsum(
        "tc,tk->ck", normed_columns, group_value, preferred_element_type=jnp.float32
    )
    group_sum = jnp.sum(group_term * full_weight.astype(jnp.float32), axis=1)
    kept_term = lax.dynamic_slice_in_dim(group_term, core * chunk, chunk, 0)
    given_term = lax.dynamic_slice_in_dim(group_term, (1 - core) * chunk, chunk, 0)
    plane_term = kept_term + other_core(given_term.astype(jnp.bfloat16)).astype(jnp.float32)
    given_back = swapped(plane_term[:, own_columns:].astype(jnp.bfloat16))
    weight_grad = (plane_term[:, :own_columns] + given_back.astype(jnp.float32)) * own_gain.astype(
        jnp.float32
    )[:, None]
    all_sums = lax.all_to_all(
        jnp.broadcast_to(group_sum[None], (2 * n_dp, 2 * chunk)), ("dp", "tensor"), 0, 0
    )
    gain_grad = jnp.sum(all_sums.reshape(n_chip, 4, 2 * chunk), axis=1).reshape(width)
    grad_hidden = finished(grad_blocks, hidden_in[0])
    to_previous = shifted(grad_hidden, "section", -1)
    return (weight_grad[None], gain_grad[None], to_previous[None])


def solution(mesh):
    placed = (
        P("section", ("dp", "tensor"), None),
        P("section", None),
        P("section", "dp", "tensor"),
        P("section", "dp", "tensor"),
        P("section", "dp", "tensor"),
        P("section", "dp", "tensor"),
        P("section", "dp"),
    )
    return jax.shard_map(
        layer,
        mesh=mesh,
        in_specs=placed,
        out_specs=(
            P("section", "dp", "tensor"),
            P("section", None),
            P("section", ("dp", "tensor"), None),
        ),
        check_vma=False,
    )
```

```python
import math

import jax
import jax.numpy as jnp
from jax import lax
from jax.experimental import pallas as pl
from jax.experimental.pallas import tpu as pltpu
from jax.sharding import PartitionSpec as P


HD = 128
QPK = 8
STEP = 16


def shifted(value, axis, steps):
    count = lax.axis_size(axis)
    first, last = (max(0, -steps), min(count, count - steps))
    return lax.ppermute(value, axis, [(source, source + steps) for source in range(first, last)])


def swapped(value):
    return lax.ppermute(value, "tensor", [(0, 1), (1, 0)])


def halfway(value):
    half = lax.axis_size("section")
    count = 2 * half
    place = [(plane % half) * 2 + plane // half for plane in range(count)]
    pairs = [(place[plane], place[(plane + half // 2) % count]) for plane in range(count)]
    return lax.ppermute(value, ("section", "tensor"), pairs)


def same_core():
    count = lax.axis_size("dp")
    return [list(range(core, count, 2)) for core in range(2)]


def exchanged(value, split, joined):
    return lax.all_to_all(value, "dp", split, joined, axis_index_groups=same_core())


def gathered(value):
    count = lax.axis_size("dp") // 2
    copies = jnp.broadcast_to(value[None], (count,) + value.shape)
    return exchanged(copies, 0, 0)


def other_core(value):
    count = lax.axis_size("dp")
    return lax.ppermute(value, "dp", [(source, source ^ 1) for source in range(count)])


def by_core(core, own, other):
    first = jnp.where(core == 0, own, other)
    second = jnp.where(core == 0, other, own)
    return jnp.concatenate([first, second], axis=0)


def whole(memory=pltpu.VMEM):
    return pl.BlockSpec(memory_space=memory)


def norm_kernel(hidden_ref, normed_ref):
    count, length, columns = normed_ref.shape
    for start in range(0, length, STEP):
        rows = pl.ds(start, STEP)
        squares = jnp.zeros((STEP, columns), jnp.float32)
        for place in range(count):
            block = hidden_ref[rows, pl.ds(place * columns, columns)].astype(jnp.float32)
            squares += block * block
        mean = jnp.sum(squares, axis=1, keepdims=True) / (count * columns)
        inverse = 1.0 / jnp.sqrt(mean + 1e-05)
        for place in range(count):
            block = hidden_ref[rows, pl.ds(place * columns, columns)].astype(jnp.float32)
            normed_ref[place, rows] = (block * inverse).astype(jnp.bfloat16)


def normed_blocks(rows, count):
    length, width = rows.shape
    return pl.pallas_call(
        norm_kernel,
        out_shape=jax.ShapeDtypeStruct((count, length, width // count), jnp.bfloat16),
        in_specs=[whole()],
        out_specs=whole(),
    )(rows)


def attend_kernel(half_ref, query_ref, key_ref, grad_ref, position_ref, kept_ref, given_ref, scratch_ref):
    length = query_ref.shape[0]
    groups = key_ref.shape[1] // HD
    seen_row = lax.broadcasted_iota(jnp.int32, (length, length), 0)
    query_row = lax.broadcasted_iota(jnp.int32, (length, length), 1)
    query_start = jnp.broadcast_to(position_ref[...], (length, length)) - query_row
    seen_start = query_start.T
    visible = (seen_row <= query_row) & (query_start == seen_start)
    for group in range(groups):
        keys = key_ref[:, group * HD : (group + 1) * HD]
        total = jnp.zeros((length, HD), jnp.float32)
        for head in range(group * QPK, (group + 1) * QPK):
            queries = query_ref[:, head * HD : (head + 1) * HD]
            scores = lax.dot_general(
                keys, queries, (((1,), (1,)), ((), ())), preferred_element_type=jnp.float32
            ) * (1.0 / math.sqrt(HD))
            masked = jnp.where(visible, scores, jnp.float32(-1e30))
            largest = jnp.max(masked, axis=0, keepdims=True)
            powers = jnp.where(visible, jnp.exp(masked - largest), jnp.float32(0.0))
            weights = powers * (1.0 / jnp.sum(powers, axis=0, keepdims=True))
            total += lax.dot_general(
                weights.astype(jnp.bfloat16),
                grad_ref[:, head * HD : (head + 1) * HD],
                (((1,), (0,)), ((), ())),
                preferred_element_type=jnp.float32,
            )
        scratch_ref[:, group * HD : (group + 1) * HD] = total
    rows = kept_ref.shape[0]
    half = half_ref[0]
    kept_ref[...] = scratch_ref[pl.ds(half * rows, rows), :].astype(jnp.bfloat16)
    given_ref[...] = scratch_ref[pl.ds((1 - half) * rows, rows), :].astype(jnp.bfloat16)


def attend(half, query_rows, key_rows, grad_rows, position_rows):
    length, columns = key_rows.shape
    part = jax.ShapeDtypeStruct((length // 2, columns), jnp.bfloat16)
    return pl.pallas_call(
        attend_kernel,
        out_shape=(part, part),
        in_specs=[whole(pltpu.SMEM)] + [whole()] * 4,
        out_specs=(whole(), whole()),
        scratch_shapes=[pltpu.VMEM((length, columns), jnp.float32)],
    )(half[None], query_rows, key_rows, grad_rows, position_rows)


def finish_kernel(grad_ref, hidden_ref, result_ref):
    count, length, columns = grad_ref.shape
    for start in range(0, length, STEP):
        rows = pl.ds(start, STEP)
        squares = jnp.zeros((STEP, columns), jnp.float32)
        total = jnp.zeros((STEP, columns), jnp.float32)
        for place in range(count):
            block = hidden_ref[rows, pl.ds(place * columns, columns)].astype(jnp.float32)
            squares += block * block
            total += grad_ref[place, rows].astype(jnp.float32) * block
        mean = jnp.sum(squares, axis=1, keepdims=True) / (count * columns)
        inverse = 1.0 / jnp.sqrt(mean + 1e-05)
        inner = jnp.sum(total, axis=1, keepdims=True) * inverse / (count * columns) * inverse
        for place in range(count):
            part = pl.ds(place * columns, columns)
            block = hidden_ref[rows, part].astype(jnp.float32)
            grads = grad_ref[place, rows].astype(jnp.float32)
            result_ref[rows, part] = ((grads - block * inner) * inverse).astype(jnp.bfloat16)


def finished(grad_blocks, rows):
    return pl.pallas_call(
        finish_kernel,
        out_shape=jax.ShapeDtypeStruct(rows.shape, jnp.bfloat16),
        in_specs=[whole(), whole()],
        out_specs=whole(),
    )(grad_blocks, rows)


def layer(hidden_in, norm_gain, value_weight, query_vectors, key_vectors, grad_attn, positions):
    n_dp = lax.axis_size("dp")
    n_chip = n_dp // 2
    here = lax.axis_index("dp")
    chip = here // 2
    core = here % 2
    half = lax.axis_index("tensor")
    own_rows, width = hidden_in.shape[1:]
    chunk = width // n_dp
    local_weight = value_weight[0]
    own_columns = local_weight.shape[1]
    normed = normed_blocks(hidden_in[0], n_chip)
    normed_columns = exchanged(normed, 0, 0).reshape(n_chip * own_rows, 2 * chunk)
    kept, given = attend(half, query_vectors[0], key_vectors[0], grad_attn[0], positions)
    own_value = jnp.concatenate([kept, swapped(given)], axis=1)
    device_weight = jnp.concatenate([local_weight, swapped(local_weight)], axis=1)
    full_weight = by_core(core, device_weight, other_core(device_weight))
    chip_gain = lax.dynamic_slice_in_dim(norm_gain[0], chip * 2 * chunk, 2 * chunk, 0)
    own_gain = lax.dynamic_slice_in_dim(norm_gain[0], here * chunk, chunk, 0)
    group_value = gathered(own_value).reshape(n_chip * own_rows, 2 * own_columns)
    grad_columns = (
        jnp.einsum("tk,ck->tc", group_value, full_weight, preferred_element_type=jnp.float32)
        * chip_gain.astype(jnp.float32)
    ).astype(jnp.bfloat16)
    grad_blocks = exchanged(grad_columns.reshape(n_chip, own_rows, 2 * chunk), 0, 0)
    group_term = jnp.einsum(
        "tc,tk->ck", normed_columns, group_value, preferred_element_type=jnp.float32
    )
    kept_term = lax.dynamic_slice_in_dim(group_term, core * chunk, chunk, 0)
    given_term = lax.dynamic_slice_in_dim(group_term, (1 - core) * chunk, chunk, 0)
    plane_term = kept_term + other_core(given_term.astype(jnp.bfloat16)).astype(jnp.float32)
    half_way = halfway(plane_term[:, own_columns:].astype(jnp.bfloat16))
    given_back = halfway(half_way)
    plane_sum = jnp.sum(plane_term * device_weight.astype(jnp.float32), axis=1)
    weight_grad = (plane_term[:, :own_columns] + given_back.astype(jnp.float32)) * own_gain.astype(
        jnp.float32
    )[:, None]
    home_sum = plane_sum + halfway(halfway(plane_sum))
    all_sums = lax.all_to_all(jnp.broadcast_to(home_sum[None], (n_dp, chunk)), "dp", 0, 0)
    gain_grad = all_sums.reshape(width)
    grad_hidden = finished(grad_blocks, hidden_in[0])
    to_previous = shifted(grad_hidden, "section", -1)
    return (weight_grad[None], gain_grad[None], to_previous[None])


def solution(mesh):
    placed = (
        P("section", ("dp", "tensor"), None),
        P("section", None),
        P("section", "dp", "tensor"),
        P("section", "dp", "tensor"),
        P("section", "dp", "tensor"),
        P("section", "dp", "tensor"),
        P("section", "dp"),
    )
    return jax.shard_map(
        layer,
        mesh=mesh,
        in_specs=placed,
        out_specs=(
            P("section", "dp", "tensor"),
            P("section", None),
            P("section", ("dp", "tensor"), None),
        ),
        check_vma=False,
    )
```

```python
import math

import jax
import jax.numpy as jnp
from jax import lax
from jax.experimental import pallas as pl
from jax.experimental.pallas import tpu as pltpu
from jax.sharding import PartitionSpec as P


HD = 128
QPK = 8
STEP = 16


def shifted(value, axis, steps):
    count = lax.axis_size(axis)
    first, last = (max(0, -steps), min(count, count - steps))
    return lax.ppermute(value, axis, [(source, source + steps) for source in range(first, last)])


def swapped(value):
    return lax.ppermute(value, "tensor", [(0, 1), (1, 0)])


def same_core():
    count = lax.axis_size("dp")
    return [list(range(core, count, 2)) for core in range(2)]


def exchanged(value, split, joined):
    return lax.all_to_all(value, "dp", split, joined, axis_index_groups=same_core())


def other_core(value):
    count = lax.axis_size("dp")
    return lax.ppermute(value, "dp", [(source, source ^ 1) for source in range(count)])


def by_core(core, own, other):
    first = jnp.where(core == 0, own, other)
    second = jnp.where(core == 0, other, own)
    return jnp.concatenate([first, second], axis=0)


def whole(memory=pltpu.VMEM):
    return pl.BlockSpec(memory_space=memory)


def spread_kernel(kept_ref, given_ref, copies_ref):
    columns = kept_ref.shape[1]
    for place in range(copies_ref.shape[0]):
        copies_ref[place, :, :columns] = kept_ref[...]
        copies_ref[place, :, columns:] = given_ref[...]


def spread(kept, given, count):
    length, columns = kept.shape
    return pl.pallas_call(
        spread_kernel,
        out_shape=jax.ShapeDtypeStruct((count, length, 2 * columns), kept.dtype),
        in_specs=[whole(), whole()],
        out_specs=whole(),
    )(kept, given)


def norm_kernel(hidden_ref, normed_ref):
    count, length, columns = normed_ref.shape
    for start in range(0, length, STEP):
        rows = pl.ds(start, STEP)
        squares = jnp.zeros((STEP, columns), jnp.float32)
        for place in range(count):
            block = hidden_ref[rows, pl.ds(place * columns, columns)].astype(jnp.float32)
            squares += block * block
        mean = jnp.sum(squares, axis=1, keepdims=True) / (count * columns)
        inverse = 1.0 / jnp.sqrt(mean + 1e-05)
        for place in range(count):
            block = hidden_ref[rows, pl.ds(place * columns, columns)].astype(jnp.float32)
            normed_ref[place, rows] = (block * inverse).astype(jnp.bfloat16)


def normed_blocks(rows, count):
    length, width = rows.shape
    return pl.pallas_call(
        norm_kernel,
        out_shape=jax.ShapeDtypeStruct((count, length, width // count), jnp.bfloat16),
        in_specs=[whole()],
        out_specs=whole(),
    )(rows)


def attend_kernel(half_ref, query_ref, key_ref, grad_ref, position_ref, kept_ref, given_ref, scratch_ref):
    length = query_ref.shape[0]
    groups = key_ref.shape[1] // HD
    seen_row = lax.broadcasted_iota(jnp.int32, (length, length), 0)
    query_row = lax.broadcasted_iota(jnp.int32, (length, length), 1)
    query_start = jnp.broadcast_to(position_ref[...], (length, length)) - query_row
    seen_start = query_start.T
    visible = (seen_row <= query_row) & (query_start == seen_start)
    for group in range(groups):
        keys = key_ref[:, group * HD : (group + 1) * HD]
        total = jnp.zeros((length, HD), jnp.float32)
        for head in range(group * QPK, (group + 1) * QPK):
            queries = query_ref[:, head * HD : (head + 1) * HD]
            scores = lax.dot_general(
                keys, queries, (((1,), (1,)), ((), ())), preferred_element_type=jnp.float32
            ) * (1.0 / math.sqrt(HD))
            masked = jnp.where(visible, scores, jnp.float32(-1e30))
            largest = jnp.max(masked, axis=0, keepdims=True)
            powers = jnp.where(visible, jnp.exp(masked - largest), jnp.float32(0.0))
            weights = powers * (1.0 / jnp.sum(powers, axis=0, keepdims=True))
            total += lax.dot_general(
                weights.astype(jnp.bfloat16),
                grad_ref[:, head * HD : (head + 1) * HD],
                (((1,), (0,)), ((), ())),
                preferred_element_type=jnp.float32,
            )
        scratch_ref[:, group * HD : (group + 1) * HD] = total
    rows = kept_ref.shape[0]
    half = half_ref[0]
    kept_ref[...] = scratch_ref[pl.ds(half * rows, rows), :].astype(jnp.bfloat16)
    given_ref[...] = scratch_ref[pl.ds((1 - half) * rows, rows), :].astype(jnp.bfloat16)


def attend(half, query_rows, key_rows, grad_rows, position_rows):
    length, columns = key_rows.shape
    part = jax.ShapeDtypeStruct((length // 2, columns), jnp.bfloat16)
    return pl.pallas_call(
        attend_kernel,
        out_shape=(part, part),
        in_specs=[whole(pltpu.SMEM)] + [whole()] * 4,
        out_specs=(whole(), whole()),
        scratch_shapes=[pltpu.VMEM((length, columns), jnp.float32)],
    )(half[None], query_rows, key_rows, grad_rows, position_rows)


def finish_kernel(grad_ref, hidden_ref, result_ref):
    count, length, columns = grad_ref.shape
    for start in range(0, length, STEP):
        rows = pl.ds(start, STEP)
        squares = jnp.zeros((STEP, columns), jnp.float32)
        total = jnp.zeros((STEP, columns), jnp.float32)
        for place in range(count):
            block = hidden_ref[rows, pl.ds(place * columns, columns)].astype(jnp.float32)
            squares += block * block
            total += grad_ref[place, rows].astype(jnp.float32) * block
        mean = jnp.sum(squares, axis=1, keepdims=True) / (count * columns)
        inverse = 1.0 / jnp.sqrt(mean + 1e-05)
        inner = jnp.sum(total, axis=1, keepdims=True) * inverse / (count * columns) * inverse
        for place in range(count):
            part = pl.ds(place * columns, columns)
            block = hidden_ref[rows, part].astype(jnp.float32)
            grads = grad_ref[place, rows].astype(jnp.float32)
            result_ref[rows, part] = ((grads - block * inner) * inverse).astype(jnp.bfloat16)


def finished(grad_blocks, rows):
    return pl.pallas_call(
        finish_kernel,
        out_shape=jax.ShapeDtypeStruct(rows.shape, jnp.bfloat16),
        in_specs=[whole(), whole()],
        out_specs=whole(),
    )(grad_blocks, rows)


def layer(hidden_in, norm_gain, value_weight, query_vectors, key_vectors, grad_attn, positions):
    n_dp = lax.axis_size("dp")
    n_chip = n_dp // 2
    here = lax.axis_index("dp")
    chip = here // 2
    core = here % 2
    half = lax.axis_index("tensor")
    own_rows, width = hidden_in.shape[1:]
    chunk = width // n_dp
    local_weight = value_weight[0]
    own_columns = local_weight.shape[1]
    normed = normed_blocks(hidden_in[0], n_chip)
    normed_columns = exchanged(normed, 0, 0).reshape(n_chip * own_rows, 2 * chunk)
    kept, given = attend(half, query_vectors[0], key_vectors[0], grad_attn[0], positions)
    own_values = spread(kept, swapped(given), n_chip)
    device_weight = jnp.concatenate([local_weight, swapped(local_weight)], axis=1)
    full_weight = by_core(core, device_weight, other_core(device_weight))
    chip_gain = lax.dynamic_slice_in_dim(norm_gain[0], chip * 2 * chunk, 2 * chunk, 0)
    own_gain = lax.dynamic_slice_in_dim(norm_gain[0], here * chunk, chunk, 0)
    group_value = exchanged(own_values, 0, 0).reshape(n_chip * own_rows, 2 * own_columns)
    grad_columns = (
        jnp.einsum("tk,ck->tc", group_value, full_weight, preferred_element_type=jnp.float32)
        * chip_gain.astype(jnp.float32)
    ).astype(jnp.bfloat16)
    grad_blocks = exchanged(grad_columns.reshape(n_chip, own_rows, 2 * chunk), 0, 0)
    group_term = jnp.einsum(
        "tc,tk->ck", normed_columns, group_value, preferred_element_type=jnp.float32
    )
    kept_term = lax.dynamic_slice_in_dim(group_term, core * chunk, chunk, 0)
    given_term = lax.dynamic_slice_in_dim(group_term, (1 - core) * chunk, chunk, 0)
    plane_term = kept_term + other_core(given_term.astype(jnp.bfloat16)).astype(
        jnp.float32
    )
    plane_sum = jnp.sum(plane_term * device_weight.astype(jnp.float32), axis=1)
    sum_high = lax.reduce_precision(plane_sum, 8, 7)
    sums = jnp.stack([sum_high, plane_sum - sum_high]).astype(jnp.bfloat16)
    sent_term = jnp.concatenate(
        [plane_term[:, own_columns:].astype(jnp.bfloat16), jnp.pad(sums, ((0, 14), (0, 0)))], axis=0
    )
    received = swapped(sent_term).astype(jnp.float32)
    given_back = received[:chunk]
    home_sum = plane_sum + received[chunk] + received[chunk + 1]
    weight_grad = (plane_term[:, :own_columns] + given_back) * own_gain.astype(
        jnp.float32
    )[:, None]
    all_sums = lax.all_to_all(jnp.broadcast_to(home_sum[None], (n_dp, chunk)), "dp", 0, 0)
    gain_grad = all_sums.reshape(width)
    grad_hidden = finished(grad_blocks, hidden_in[0])
    to_previous = shifted(grad_hidden, "section", -1)
    return (weight_grad[None], gain_grad[None], to_previous[None])


def solution(mesh):
    placed = (
        P("section", ("dp", "tensor"), None),
        P("section", None),
        P("section", "dp", "tensor"),
        P("section", "dp", "tensor"),
        P("section", "dp", "tensor"),
        P("section", "dp", "tensor"),
        P("section", "dp"),
    )
    return jax.shard_map(
        layer,
        mesh=mesh,
        in_specs=placed,
        out_specs=(
            P("section", "dp", "tensor"),
            P("section", None),
            P("section", ("dp", "tensor"), None),
        ),
        check_vma=False,
    )
```

```python
import math

import jax
import jax.numpy as jnp
from jax import lax
from jax.experimental import pallas as pl
from jax.experimental.pallas import tpu as pltpu
from jax.sharding import PartitionSpec as P


HD = 128
QPK = 8
STEP = 16


def shifted(value, axis, steps):
    count = lax.axis_size(axis)
    first, last = (max(0, -steps), min(count, count - steps))
    return lax.ppermute(value, axis, [(source, source + steps) for source in range(first, last)])


def swapped(value):
    return lax.ppermute(value, "tensor", [(0, 1), (1, 0)])


def same_core():
    count = lax.axis_size("dp")
    return [list(range(core, count, 2)) for core in range(2)]


def exchanged(value, split, joined):
    return lax.all_to_all(value, "dp", split, joined, axis_index_groups=same_core())


def gathered(value):
    count = lax.axis_size("dp") // 2
    copies = jnp.broadcast_to(value[None], (count,) + value.shape)
    return exchanged(copies, 0, 0)


def other_core(value):
    count = lax.axis_size("dp")
    return lax.ppermute(value, "dp", [(source, source ^ 1) for source in range(count)])


def by_core(core, own, other):
    first = jnp.where(core == 0, own, other)
    second = jnp.where(core == 0, other, own)
    return jnp.concatenate([first, second], axis=0)


def whole(memory=pltpu.VMEM):
    return pl.BlockSpec(memory_space=memory)


def norm_kernel(hidden_ref, normed_ref):
    count, length, columns = normed_ref.shape
    for start in range(0, length, STEP):
        rows = pl.ds(start, STEP)
        squares = jnp.zeros((STEP, columns), jnp.float32)
        for place in range(count):
            block = hidden_ref[rows, pl.ds(place * columns, columns)].astype(jnp.float32)
            squares += block * block
        mean = jnp.sum(squares, axis=1, keepdims=True) / (count * columns)
        inverse = 1.0 / jnp.sqrt(mean + 1e-05)
        for place in range(count):
            block = hidden_ref[rows, pl.ds(place * columns, columns)].astype(jnp.float32)
            normed_ref[place, rows] = (block * inverse).astype(jnp.bfloat16)


def normed_blocks(rows, count):
    length, width = rows.shape
    return pl.pallas_call(
        norm_kernel,
        out_shape=jax.ShapeDtypeStruct((count, length, width // count), jnp.bfloat16),
        in_specs=[whole()],
        out_specs=whole(),
    )(rows)


def attend_kernel(half_ref, query_ref, key_ref, grad_ref, position_ref, kept_ref, given_ref, scratch_ref):
    length = query_ref.shape[0]
    groups = key_ref.shape[1] // HD
    seen_row = lax.broadcasted_iota(jnp.int32, (length, length), 0)
    query_row = lax.broadcasted_iota(jnp.int32, (length, length), 1)
    query_start = jnp.broadcast_to(position_ref[...], (length, length)) - query_row
    seen_start = query_start.T
    visible = (seen_row <= query_row) & (query_start == seen_start)
    for group in range(groups):
        keys = key_ref[:, group * HD : (group + 1) * HD]
        total = jnp.zeros((length, HD), jnp.float32)
        for head in range(group * QPK, (group + 1) * QPK):
            queries = query_ref[:, head * HD : (head + 1) * HD]
            scores = lax.dot_general(
                keys, queries, (((1,), (1,)), ((), ())), preferred_element_type=jnp.float32
            ) * (1.0 / math.sqrt(HD))
            masked = jnp.where(visible, scores, jnp.float32(-1e30))
            largest = jnp.max(masked, axis=0, keepdims=True)
            powers = jnp.where(visible, jnp.exp(masked - largest), jnp.float32(0.0))
            weights = powers * (1.0 / jnp.sum(powers, axis=0, keepdims=True))
            total += lax.dot_general(
                weights.astype(jnp.bfloat16),
                grad_ref[:, head * HD : (head + 1) * HD],
                (((1,), (0,)), ((), ())),
                preferred_element_type=jnp.float32,
            )
        scratch_ref[:, group * HD : (group + 1) * HD] = total
    rows = kept_ref.shape[0]
    half = half_ref[0]
    kept_ref[...] = scratch_ref[pl.ds(half * rows, rows), :].astype(jnp.bfloat16)
    given_ref[...] = scratch_ref[pl.ds((1 - half) * rows, rows), :].astype(jnp.bfloat16)


def attend(half, query_rows, key_rows, grad_rows, position_rows):
    length, columns = key_rows.shape
    part = jax.ShapeDtypeStruct((length // 2, columns), jnp.bfloat16)
    return pl.pallas_call(
        attend_kernel,
        out_shape=(part, part),
        in_specs=[whole(pltpu.SMEM)] + [whole()] * 4,
        out_specs=(whole(), whole()),
        scratch_shapes=[pltpu.VMEM((length, columns), jnp.float32)],
    )(half[None], query_rows, key_rows, grad_rows, position_rows)


def finish_kernel(grad_ref, hidden_ref, result_ref):
    count, length, columns = grad_ref.shape
    for start in range(0, length, STEP):
        rows = pl.ds(start, STEP)
        squares = jnp.zeros((STEP, columns), jnp.float32)
        total = jnp.zeros((STEP, columns), jnp.float32)
        for place in range(count):
            block = hidden_ref[rows, pl.ds(place * columns, columns)].astype(jnp.float32)
            squares += block * block
            total += grad_ref[place, rows].astype(jnp.float32) * block
        mean = jnp.sum(squares, axis=1, keepdims=True) / (count * columns)
        inverse = 1.0 / jnp.sqrt(mean + 1e-05)
        inner = jnp.sum(total, axis=1, keepdims=True) * inverse / (count * columns) * inverse
        for place in range(count):
            part = pl.ds(place * columns, columns)
            block = hidden_ref[rows, part].astype(jnp.float32)
            grads = grad_ref[place, rows].astype(jnp.float32)
            result_ref[rows, part] = ((grads - block * inner) * inverse).astype(jnp.bfloat16)


def finished(grad_blocks, rows):
    return pl.pallas_call(
        finish_kernel,
        out_shape=jax.ShapeDtypeStruct(rows.shape, jnp.bfloat16),
        in_specs=[whole(), whole()],
        out_specs=whole(),
    )(grad_blocks, rows)


def layer(hidden_in, norm_gain, value_weight, query_vectors, key_vectors, grad_attn, positions):
    n_dp = lax.axis_size("dp")
    n_chip = n_dp // 2
    here = lax.axis_index("dp")
    chip = here // 2
    core = here % 2
    half = lax.axis_index("tensor")
    own_rows, width = hidden_in.shape[1:]
    chunk = width // n_dp
    local_weight = value_weight[0]
    own_columns = local_weight.shape[1]
    normed = normed_blocks(hidden_in[0], n_chip)
    normed_columns = exchanged(normed, 0, 0).reshape(n_chip * own_rows, 2 * chunk)
    kept, given = attend(half, query_vectors[0], key_vectors[0], grad_attn[0], positions)
    own_value = jnp.concatenate([kept, swapped(given)], axis=1)
    device_weight = jnp.concatenate([local_weight, swapped(local_weight)], axis=1)
    full_weight = by_core(core, device_weight, other_core(device_weight))
    chip_gain = lax.dynamic_slice_in_dim(norm_gain[0], chip * 2 * chunk, 2 * chunk, 0)
    own_gain = lax.dynamic_slice_in_dim(norm_gain[0], here * chunk, chunk, 0)
    group_value = gathered(own_value).reshape(n_chip * own_rows, 2 * own_columns)
    grad_columns = (
        jnp.einsum("tk,ck->tc", group_value, full_weight, preferred_element_type=jnp.float32)
        * chip_gain.astype(jnp.float32)
    ).astype(jnp.bfloat16)
    grad_blocks = exchanged(grad_columns.reshape(n_chip, own_rows, 2 * chunk), 0, 0)
    group_term = jnp.einsum(
        "tc,tk->ck", normed_columns, group_value, preferred_element_type=jnp.float32
    )
    kept_term = lax.dynamic_slice_in_dim(group_term, core * chunk, chunk, 0)
    given_term = lax.dynamic_slice_in_dim(group_term, (1 - core) * chunk, chunk, 0)
    plane_term = kept_term + other_core(given_term.astype(jnp.bfloat16)).astype(
        jnp.float32
    )
    plane_sum = jnp.sum(plane_term * device_weight.astype(jnp.float32), axis=1)
    sum_high = lax.reduce_precision(plane_sum, 8, 7)
    sums = jnp.stack([sum_high, plane_sum - sum_high]).astype(jnp.bfloat16)
    sent_term = jnp.concatenate(
        [plane_term[:, own_columns:].astype(jnp.bfloat16), jnp.pad(sums, ((0, 14), (0, 0)))], axis=0
    )
    received = swapped(sent_term).astype(jnp.float32)
    given_back = received[:chunk]
    home_sum = plane_sum + received[chunk] + received[chunk + 1]
    weight_grad = (plane_term[:, :own_columns] + given_back) * own_gain.astype(
        jnp.float32
    )[:, None]
    all_sums = lax.all_to_all(jnp.broadcast_to(home_sum[None], (n_dp, chunk)), "dp", 0, 0)
    gain_grad = all_sums.reshape(width)
    grad_hidden = finished(grad_blocks, hidden_in[0])
    to_previous = shifted(grad_hidden, "section", -1)
    return (weight_grad[None], gain_grad[None], to_previous[None])


def solution(mesh):
    placed = (
        P("section", ("dp", "tensor"), None),
        P("section", None),
        P("section", "dp", "tensor"),
        P("section", "dp", "tensor"),
        P("section", "dp", "tensor"),
        P("section", "dp", "tensor"),
        P("section", "dp"),
    )
    return jax.shard_map(
        layer,
        mesh=mesh,
        in_specs=placed,
        out_specs=(
            P("section", "dp", "tensor"),
            P("section", None),
            P("section", ("dp", "tensor"), None),
        ),
        check_vma=False,
    )
```
